128 devices in a mesh: grp: 2 (over y_lo), tp: 64 (over y_hi, z, x, core).
Axes of the slice: x: 4, y: 4 (y_hi: 2, y_lo: 2; y = y_hi * 2 + y_lo), z: 4, core: 2. Of those that a mesh axis runs over, the one named last changes fastest.
Arguments:
- patches: bfloat16 [5120, 1408], P('tp'), may hold values from -6 to 6
- grids: int32 [64, 3, 2], P('tp'), may hold values from 0 to 40, as said below
- positions: int32 [1280], replicated, may hold values from 0 to 2048, as said below
- vis_gain: float32 [1408], replicated, may hold values from 0.1 to 1.9
- vis_query: bfloat16 [1408, 1408], P(None, 'grp')
- vis_key: bfloat16 [1408, 1408], P(None, 'grp'), may hold values from -0.15625 to 0.15625
- vis_value: bfloat16 [1408, 1408], P(None, 'grp'), may hold values from -0.15625 to 0.15625
- vis_out: bfloat16 [1408, 1408], P('grp'), may hold values from -0.15625 to 0.15625
- w_proj: bfloat16 [5632, 4096], P(None, 'tp'), may hold values from -0.078125 to 0.078125
- text_embed: bfloat16 [2048, 4096], P(('grp', 'tp')), may hold values from -6 to 6
- slots: int32 [2, 512], P('grp'), may hold values from 0 to 1023, as said below
- lengths: int32 [2, 8], P('grp'), may hold values from 1 to 256, 1024 in all within a row
- attn_gain: float32 [4096], replicated, may hold values from 0.1 to 1.9
- mlp_gain: float32 [4096], replicated, may hold values from 0.1 to 1.9
- w_kv: bfloat16 [4096, 8192], P(None, 'tp'), may hold values from -0.09375 to 0.09375
- w_gate: bfloat16 [4096, 11008], P(None, 'tp'), may hold values from -0.09375 to 0.09375
- w_up: bfloat16 [4096, 11008], P(None, 'tp'), may hold values from -0.09375 to 0.09375
- w_down: bfloat16 [11008, 4096], P('tp'), may hold values from -0.0546875 to 0.0546875
Outputs:
- layer_out: bfloat16 [2048, 4096], P(('grp', 'tp'))
- kv_out: bfloat16 [2, 512, 8192], P('grp', None, 'tp')
The draws below stay inside these ranges and needn't reach their ends.
Inputs may be any that keep to these rules, and one draw needn't show every extreme that they name: `grids`: heights and widths are even; the areas of one tp index sum to at most 80; a height of 0 marks an empty entry. `positions`: every merged cell slot inside an image holds a distinct prompt position below 2048, increasing with the slot; slots past a block's images hold 2048. `slots`: distinct within each batch.
All inputs are finite; a program needn't handle non-finite values.
Results may differ from the reference program's by a relative error of at most 0.014.
The reference program's roundings to bfloat16 on the way count: a program that leaves them out, or rounds other values in their place, can miss the bound.
Values may be sent and summed in bfloat16 or wider, within the bound.
A program may use at most 128 MiB of HBM per device.

```python
import math
import jax
import jax.numpy as jnp
import numpy as np
from jax import lax

VD = 1408
VH = 16
VHD = 88
D = 4096
HD = 128
FF = 11008
VMERGE = 5632
PATCH_DEV = 80
MERGE_DEV = 20
IMGS = 3
REQS = 8
PATCHES = 5120
MERGED = 1280
TOKENS = 2048
HALF_TOK = 1024
SLOT_HALF = 512
LEN_MOST = 256
N_GRP = 2
N_TP = 64


def put_first(perm_ids, wanted):
    where_wanted = jnp.argmax((perm_ids == wanted).astype(jnp.int32))
    first_value = perm_ids[0]
    return perm_ids.at[where_wanted].set(first_value).at[0].set(wanted)


def image_layout(key):
    layout_key = jax.random.fold_in(key, 17)
    key_sides, key_fill = jax.random.split(layout_key)
    sides = jax.random.randint(key_sides, (N_TP, IMGS - 1, 2), 1, 4)
    fills = jax.random.randint(key_fill, (N_TP,), MERGE_DEV // 4, MERGE_DEV + 1)
    device_ids = jnp.arange(N_TP)
    fills = jnp.where(device_ids == 0, MERGE_DEV, jnp.where(device_ids == 1, MERGE_DEV // 4, fills))
    areas = sides[:, :, 0] * sides[:, :, 1]
    keeping = (jnp.cumsum(areas, axis=1) <= fills[:, None]) & (device_ids[:, None] != 0)
    heights = jnp.where(keeping, 2 * sides[:, :, 0], 0)
    widths = jnp.where(keeping, 2 * sides[:, :, 1], 2)
    remain = fills - jnp.sum(jnp.where(keeping, areas, 0), axis=1)
    heights = jnp.concatenate([heights, 2 * remain[:, None]], axis=1)
    widths = jnp.concatenate([widths, jnp.full((N_TP, 1), 2, jnp.int32)], axis=1)
    return (jnp.stack([heights, widths], axis=2).astype(jnp.int32), fills)


def draw_grids(key, part):
    return image_layout(key)[0]


def draw_positions(key, part):
    layout_grids, fills = image_layout(key)
    cell_ids = jnp.arange(MERGE_DEV)
    valid = (cell_ids[None, :] < fills[:, None]).reshape(-1)
    rank = jnp.cumsum(valid.astype(jnp.int32)) - 1
    perm_ids = put_first(jax.random.permutation(jax.random.fold_in(key, 29), TOKENS), 0)
    chosen = jnp.sort(perm_ids[:MERGED])
    return jnp.where(valid, chosen[jnp.clip(rank, 0, MERGED - 1)], TOKENS).astype(jnp.int32)


def draw_slots(key, part):
    slot_keys = jax.random.split(jax.random.fold_in(key, 41), N_GRP)
    picked = []
    for batch_index in range(N_GRP):
        perm_ids = jax.random.permutation(slot_keys[batch_index], HALF_TOK)
        perm_ids = put_first(perm_ids, HALF_TOK - 1)
        tail_ids = perm_ids[1:]
        zero_at = jnp.argmax((tail_ids == 0).astype(jnp.int32))
        tail_ids = tail_ids.at[zero_at].set(tail_ids[0]).at[0].set(0)
        perm_ids = jnp.concatenate([perm_ids[:1], tail_ids])
        picked.append(perm_ids[:SLOT_HALF])
    return jnp.stack(picked).astype(jnp.int32)


def draw_vis_query(key, part):
    base = jax.random.normal(jax.random.fold_in(key, 53), (VD, VD), jnp.float32) * VD ** (-0.5)
    return base.astype(jnp.bfloat16)


def shard_levels(own_key, extent, pieces, low, top_value):
    level, own = 1.0, jax.random.fold_in(own_key, 6)
    for position, parts in pieces:
        steps = jnp.exp(jax.random.uniform(jax.random.fold_in(own, position), (parts,), jnp.float32, low / len(pieces), top_value / len(pieces)))
        level = level * jnp.repeat(steps, extent[position] // parts).reshape([-1 if axis == position else 1 for axis in range(len(extent))])
    return level


def split_up(amount, total, limit, skew):
    portions = [(1 << 20) // math.isqrt(standing ** skew) + 1 for standing in range(2, amount + 1)]
    spare, counts = total - limit - (amount - 1), [1] * (amount - 1)
    while spare > 0:
        candidates = [i for i in range(amount - 1) if counts[i] < limit]
        mass, remaining = sum([portions[i] for i in candidates]), spare
        for i in candidates:
            addition = min(limit - counts[i], max(1, remaining * portions[i] // mass), spare)
            counts[i] = counts[i] + addition
            spare = spare - addition
    return np.array([limit] + counts)


def ragged(rng, count, total, reach, lean):
    if count == 2:
        one = jax.random.randint(rng, (), max(1, total - reach), min(reach, total - 1) + 1)
        return jnp.stack([one, total - one])
    tallies = jnp.asarray(split_up(count, total, reach, lean), jnp.int32)
    pairs = (count - 1) // 2
    donor, receiver = tallies[1:1 + 2 * pairs:2], tallies[2:2 + 2 * pairs:2]
    slack = jnp.minimum(donor - 1, reach - receiver)
    moved = jax.random.randint(jax.random.fold_in(rng, 1), (pairs,), 0, 1 << 20) % (slack + 1)
    tallies = tallies.at[1:1 + 2 * pairs:2].set(donor - moved).at[2:2 + 2 * pairs:2].set(receiver + moved)
    return tallies[jax.random.permutation(jax.random.fold_in(rng, 2), count)]


def normal_values(key, shape, scale, most, pieces=(), kind=jnp.bfloat16):
    loudness = shard_levels(key, shape, pieces, -0.22, 0.18) if pieces else 1.0
    array = jax.random.normal(key, shape, jnp.float32) * scale * loudness
    return jnp.minimum(jnp.maximum(array, -most), most).astype(kind)


def setup_inputs(seed: int = 0) -> dict:
    key_of = jax.random.split(jax.random.key(seed), 19)
    patches = normal_values(key_of[0], (PATCHES, VD), 1.0, 6.0, ((0, 64),))
    grids = draw_grids(jax.random.fold_in(key_of[18], 71), 0)
    positions = draw_positions(jax.random.fold_in(key_of[18], 71), 0)
    vis_gain = jnp.clip(1.0 + 0.18 * jax.random.normal(key_of[3], (VD,), jnp.float32), 0.1, 1.9)
    vis_query = draw_vis_query(jax.random.fold_in(key_of[18], 71), 0)
    vis_key = normal_values(key_of[5], (VD, VD), VD ** -0.5, 0.15625, ((1, 2),))
    vis_value = normal_values(key_of[6], (VD, VD), VD ** -0.5, 0.15625, ((1, 2),))
    vis_out = normal_values(key_of[7], (VD, VD), VD ** -0.5, 0.15625, ((0, 2),))
    w_proj = normal_values(key_of[8], (VMERGE, D), VMERGE ** -0.5, 0.078125, ((1, 64),))
    text_embed = normal_values(key_of[9], (TOKENS, D), 1.0, 6.0, ((0, 128),))
    slots = draw_slots(jax.random.fold_in(key_of[18], 71), 0)
    lengths = jax.vmap(lambda own: ragged(own, REQS, HALF_TOK, LEN_MOST, 2))(jax.random.split(key_of[11], N_GRP)).reshape((N_GRP, REQS)).astype(jnp.int32)
    attn_gain = jnp.clip(1.0 + 0.18 * jax.random.normal(key_of[12], (D,), jnp.float32), 0.1, 1.9)
    mlp_gain = jnp.clip(1.0 + 0.18 * jax.random.normal(key_of[13], (D,), jnp.float32), 0.1, 1.9)
    w_kv = normal_values(key_of[14], (D, 2 * D), D ** -0.5, 0.09375, ((1, 64),))
    w_gate = normal_values(key_of[15], (D, FF), D ** -0.5, 0.09375, ((1, 64),))
    w_up = normal_values(key_of[16], (D, FF), D ** -0.5, 0.09375, ((1, 64),))
    w_down = normal_values(key_of[17], (FF, D), FF ** -0.5, 0.0546875, ((0, 64),))
    return {"patches": patches, "grids": grids, "positions": positions, "vis_gain": vis_gain, "vis_query": vis_query, "vis_key": vis_key, "vis_value": vis_value, "vis_out": vis_out, "w_proj": w_proj, "text_embed": text_embed, "slots": slots, "lengths": lengths, "attn_gain": attn_gain, "mlp_gain": mlp_gain, "w_kv": w_kv, "w_gate": w_gate, "w_up": w_up, "w_down": w_down}


def layer_norm(row_data, gain_vec):
    as_float = row_data.astype(jnp.float32)
    center = as_float - lax.optimization_barrier(jnp.mean(as_float, axis=-1, keepdims=True))
    spread = lax.optimization_barrier(jnp.mean(center * center, axis=-1, keepdims=True))
    return (center * lax.rsqrt(spread + 1e-06) * gain_vec.astype(jnp.float32)).astype(jnp.bfloat16)

def rms_norm(row_data, gain_vec):
    as_float = row_data.astype(jnp.float32)
    square_mean = lax.optimization_barrier(jnp.mean(as_float * as_float, axis=-1, keepdims=True))
    return (as_float * lax.rsqrt(square_mean + 1e-05) * gain_vec.astype(jnp.float32)).astype(jnp.bfloat16)

def image_tables(grid_dev):
    heights = grid_dev[:, 0]
    widths = grid_dev[:, 1]
    areas = heights * widths
    seg_ends = jnp.cumsum(areas)
    slot_ids = jnp.arange(PATCH_DEV, dtype=jnp.int32)
    segment = lax.optimization_barrier(jnp.sum((slot_ids[:, None] >= seg_ends[None, :]).astype(jnp.int32), axis=1))
    cell_areas = areas // 4
    cell_ends = jnp.cumsum(cell_areas)
    cell_starts = cell_ends - cell_areas
    cell_ids = jnp.arange(MERGE_DEV, dtype=jnp.int32)
    which = lax.optimization_barrier(jnp.sum((cell_ids[:, None] >= cell_ends[None, :]).astype(jnp.int32), axis=1))
    which = jnp.minimum(which, IMGS - 1)
    select = (which[:, None] == jnp.arange(IMGS, dtype=jnp.int32)[None, :]).astype(jnp.int32)
    start_cell = lax.optimization_barrier(jnp.sum(select * cell_starts[None, :], axis=1))
    width_sel = lax.optimization_barrier(jnp.sum(select * widths[None, :], axis=1))
    half_width = jnp.maximum(width_sel // 2, 1)
    inner = cell_ids - start_cell
    row_pair = inner // half_width
    col_pair = inner % half_width
    corner = 4 * start_cell + 2 * row_pair * width_sel + 2 * col_pair
    corners = jnp.stack([corner, corner + 1, corner + width_sel, corner + width_sel + 1], axis=1)
    valid = cell_ids < cell_ends[IMGS - 1]
    return (segment, jnp.where(valid[:, None], corners, 0).astype(jnp.int32))

def vision_block(row_data, grid_dev, vis_gain, vis_query, vis_key, vis_value, vis_out):
    segment, corners = image_tables(grid_dev)
    normed = layer_norm(row_data, vis_gain)
    query_rows = jnp.dot(normed, vis_query, preferred_element_type=jnp.float32).astype(jnp.bfloat16)
    key_rows = jnp.dot(normed, vis_key, preferred_element_type=jnp.float32).astype(jnp.bfloat16)
    value_rows = jnp.dot(normed, vis_value, preferred_element_type=jnp.float32).astype(jnp.bfloat16)
    slot_count = row_data.shape[0]
    head_query = query_rows.astype(jnp.float32).reshape(slot_count, VH, VHD)
    head_key = key_rows.astype(jnp.float32).reshape(slot_count, VH, VHD)
    head_value = value_rows.astype(jnp.float32).reshape(slot_count, VH, VHD)
    scores = jnp.einsum('qhd,khd->hqk', head_query, head_key) * VHD ** (-0.5)
    allowed = segment[:, None] == segment[None, :]
    scores = jnp.where(allowed[None, :, :], scores, -1e+30)
    row_max = lax.optimization_barrier(jnp.max(scores, axis=-1, keepdims=True))
    expos = jnp.exp(scores - row_max)
    attn_probs = (expos / lax.optimization_barrier(jnp.sum(expos, axis=-1, keepdims=True))).astype(jnp.bfloat16)
    context = jnp.einsum('hqk,khd->qhd', attn_probs.astype(jnp.float32), head_value)
    context = context.reshape(slot_count, VD).astype(jnp.bfloat16)
    attended = jnp.dot(context, vis_out, preferred_element_type=jnp.float32)
    vision = (row_data.astype(jnp.float32) + attended).astype(jnp.bfloat16)
    return vision[corners.reshape(-1)].reshape(MERGE_DEV, 4 * VD)

def rotate_keys(values_f, token_pos, first_col):
    col_count = values_f.shape[1]
    col_ids = first_col + jnp.arange(0, col_count, 2, dtype=jnp.int32)
    pair_ids = col_ids % HD // 2
    is_key = col_ids // HD % 2 == 0
    freq = jnp.exp(pair_ids.astype(jnp.float32) * (-2.0 * math.log(10000.0) / HD))
    angle = token_pos.astype(jnp.float32)[:, None] * freq[None, :]
    cosine = jnp.where(is_key[None, :], jnp.cos(angle), 1.0)
    sine = jnp.where(is_key[None, :], jnp.sin(angle), 0.0)
    paired = values_f.reshape(values_f.shape[0], col_count // 2, 2)
    even_part = paired[:, :, 0]
    odd_part = paired[:, :, 1]
    turned = jnp.stack([even_part * cosine - odd_part * sine, even_part * sine + odd_part * cosine], axis=2)
    return turned.reshape(values_f.shape[0], col_count)

def slot_positions(slot_ids, length_row):
    req_ends = jnp.cumsum(length_row)
    req_starts = req_ends - length_row
    inside = (slot_ids[:, None] >= req_starts[None, :]) & (slot_ids[:, None] < req_ends[None, :])
    return slot_ids - lax.optimization_barrier(jnp.sum(jnp.where(inside, req_starts[None, :], 0), axis=1))

def reference(patches, grids, positions, vis_gain, vis_query, vis_key, vis_value, vis_out, w_proj, text_embed, slots, lengths, attn_gain, mlp_gain, w_kv, w_gate, w_up, w_down):
    blocks = patches.reshape(N_TP, PATCH_DEV, VD)

    def one_block(block_pair):
        return vision_block(block_pair[0], block_pair[1], vis_gain, vis_query, vis_key, vis_value, vis_out)
    merged = lax.map(one_block, (blocks, grids)).reshape(MERGED, VMERGE)
    projected = jnp.dot(merged, w_proj, preferred_element_type=jnp.float32).astype(jnp.bfloat16)
    assembled = text_embed.at[positions].set(projected, mode='drop')
    mlp_normed = rms_norm(assembled, mlp_gain)
    gate_val = jnp.dot(mlp_normed, w_gate, preferred_element_type=jnp.float32)
    up_val = jnp.dot(mlp_normed, w_up, preferred_element_type=jnp.float32)
    hidden = (jax.nn.silu(gate_val) * up_val).astype(jnp.bfloat16)
    mixed = jnp.dot(hidden, w_down, preferred_element_type=jnp.float32)
    layer_out = (assembled.astype(jnp.float32) + mixed).astype(jnp.bfloat16)
    kv_list = []
    for batch_index in range(N_GRP):
        token_batch = assembled[batch_index * HALF_TOK:(batch_index + 1) * HALF_TOK]
        slot_rows = token_batch[slots[batch_index]]
        attn_normed = rms_norm(slot_rows, attn_gain)
        kv_full = jnp.dot(attn_normed, w_kv, preferred_element_type=jnp.float32)
        token_pos = slot_positions(slots[batch_index], lengths[batch_index])
        kv_list.append(rotate_keys(kv_full, token_pos, 0).astype(jnp.bfloat16))
    return (layer_out, jnp.stack(kv_list))
```

```python
import math

import jax
import jax.numpy as jnp
from jax import lax
from jax.experimental import pallas as pl
from jax.experimental.pallas import tpu as pltpu
from jax.sharding import PartitionSpec as P

VHD = 88
HD = 128
PATCH_DEV = 80
MERGE_DEV = 20
IMGS = 3


def layer_norm(row_data, gain_vec):
    as_float = row_data.astype(jnp.float32)
    center = as_float - jnp.mean(as_float, axis=-1, keepdims=True)
    spread = jnp.mean(center * center, axis=-1, keepdims=True)
    return (center * lax.rsqrt(spread + 1e-06) * gain_vec).astype(jnp.bfloat16)


def rms_norm(row_data, gain_vec):
    as_float = row_data.astype(jnp.float32)
    square_mean = jnp.mean(as_float * as_float, axis=-1, keepdims=True)
    return (as_float * lax.rsqrt(square_mean + 1e-05) * gain_vec).astype(jnp.bfloat16)


def image_tables(grid_dev):
    heights = grid_dev[:, 0]
    widths = grid_dev[:, 1]
    areas = heights * widths
    seg_ends = jnp.cumsum(areas)
    slot_ids = jnp.arange(PATCH_DEV, dtype=jnp.int32)
    segment = jnp.sum((slot_ids[:, None] >= seg_ends[None, :]).astype(jnp.int32), axis=1)
    cell_areas = areas // 4
    cell_ends = jnp.cumsum(cell_areas)
    cell_starts = cell_ends - cell_areas
    cell_ids = jnp.arange(MERGE_DEV, dtype=jnp.int32)
    which = jnp.sum((cell_ids[:, None] >= cell_ends[None, :]).astype(jnp.int32), axis=1)
    which = jnp.minimum(which, IMGS - 1)
    select = (which[:, None] == jnp.arange(IMGS, dtype=jnp.int32)[None, :]).astype(jnp.int32)
    start_cell = jnp.sum(select * cell_starts[None, :], axis=1)
    width_sel = jnp.sum(select * widths[None, :], axis=1)
    half_width = jnp.maximum(width_sel // 2, 1)
    inner = cell_ids - start_cell
    row_pair = inner // half_width
    col_pair = inner % half_width
    corner = 4 * start_cell + 2 * row_pair * width_sel + 2 * col_pair
    corners = jnp.stack([corner, corner + 1, corner + width_sel, corner + width_sel + 1], axis=1)
    valid = cell_ids < cell_ends[IMGS - 1]
    return (segment, jnp.where(valid[:, None], corners, 0))


def rotation_tables(token_pos):
    pair_ids = jnp.arange(HD, dtype=jnp.int32) // 2
    freq = jnp.exp(pair_ids.astype(jnp.float32) * (-2.0 * math.log(10000.0) / HD))
    angle = token_pos.astype(jnp.float32)[:, None] * freq[None, :]
    odd = jnp.arange(HD, dtype=jnp.int32)[None, :] % 2 == 1
    sine = jnp.sin(angle)
    return jnp.cos(angle), jnp.where(odd, sine, -sine)


def slot_positions(slot_ids, length_row):
    req_ends = jnp.cumsum(length_row)
    req_starts = req_ends - length_row
    inside = (slot_ids[:, None] >= req_starts[None, :]) & (slot_ids[:, None] < req_ends[None, :])
    return slot_ids - jnp.sum(jnp.where(inside, req_starts[None, :], 0), axis=1)


MESH = pl.DeviceIdType.MESH
BF = jnp.bfloat16
F32 = jnp.float32
D = 4096
UNITS = 172
CHIPS = 32
ROWS = 512
OWN = 16
STEP = 1024


class Place:
    def __init__(self):
        index = lax.axis_index("tp")
        self.core = lax.rem(index, 2)
        self.x = lax.rem(lax.div(index, 2), 4)
        self.z = lax.rem(lax.div(index, 8), 4)
        self.yh = lax.div(index, 32)

    def chip(self, far, dz, dx):
        yh = 1 - self.yh if far else self.yh
        return (yh * 4 + lax.rem(self.z + dz + 4, 4)) * 4 + lax.rem(self.x + dx + 4, 4)

    def device(self, far, dz, dx, other_core=False):
        core = 1 - self.core if other_core else self.core
        return self.chip(far, dz, dx) * 2 + core

    def along(self, order, far, first, second):
        return self.chip(far, second, first) if order == 0 else self.chip(far, first, second)

    def step(self, order, stage, sign):
        along_x = (order == 0) == (stage == 0)
        return self.device(False, 0, sign) if along_x else self.device(False, sign, 0)


def greet(place):
    barrier = pltpu.get_barrier_semaphore()
    peers = [
        place.device(False, 0, 1),
        place.device(False, 0, -1),
        place.device(False, 1, 0),
        place.device(False, -1, 0),
        place.device(True, 0, 0),
        place.device(False, 0, 0, other_core=True),
    ]
    for peer in peers:
        pl.semaphore_signal(barrier, inc=1, device_id={"tp": peer}, device_id_type=MESH)
    pl.semaphore_wait(barrier, len(peers))


class Mail:
    def __init__(self, send_sems, recv_sems):
        self.send_sems = send_sems
        self.recv_sems = recv_sems
        self.sent = []

    def send(self, src, dst, peer):
        number = len(self.sent)
        copy = pltpu.make_async_remote_copy(
            src_ref=src,
            dst_ref=dst,
            send_sem=self.send_sems.at[number],
            recv_sem=self.recv_sems.at[number],
            device_id={"tp": peer},
            device_id_type=MESH,
        )
        copy.start()
        self.sent.append(copy)
        return copy

    def finish(self):
        for copy in self.sent:
            copy.wait_send()


class Gather:
    def __init__(self, place, mail, view, whole):
        self.place, self.mail, self.view, self.whole = place, mail, view, whole

    def pair_start(self):
        ref = self.whole(self.place.chip(False, 0, 0))
        self.pair = self.mail.send(ref, ref, self.place.device(True, 0, 0))

    def pair_wait(self):
        self.pair.wait_recv()

    def pass_on(self, order, far, first, second, quarter, stage, sign):
        ref = self.view(self.place.along(order, far, first, second), order, quarter)
        return self.mail.send(ref, ref, self.place.step(order, stage, sign))

    def open(self, far):
        state = {}
        for order in (0, 1):
            for sign in (1, -1):
                state[order, 0, sign] = self.pass_on(order, far, 0, 0, None, 0, sign)
        for order in (0, 1):
            self.spread(state, order, far, 0)
        return state

    def spread(self, state, order, far, first):
        for sign in (1, -1):
            state[order, 1, first, sign] = self.pass_on(order, far, first, 0, None, 1, sign)

    def near(self, state, far):
        for order in (0, 1):
            for sign, quarter in ((1, 0), (-1, 1)):
                state[order, 0, sign].wait_recv()
                state[order, 2, sign] = self.pass_on(order, far, -sign, 0, quarter, 0, sign)
        for order in (0, 1):
            self.spread(state, order, far, 1)
            self.spread(state, order, far, -1)

    def opposite(self, state, far):
        for order in (0, 1):
            for sign in (1, -1):
                state[order, 2, sign].wait_recv()
        for order in (0, 1):
            self.spread(state, order, far, 2)

    def relay(self, state, far, first):
        for order in (0, 1):
            for sign, quarter in ((1, 0), (-1, 1)):
                state[order, 1, first, sign].wait_recv()
                state[order, 3, first, sign] = self.pass_on(
                    order, far, first, -sign, quarter, 1, sign
                )

    def close(self, state):
        for order in (0, 1):
            for first in (0, 1, -1, 2):
                for sign in (1, -1):
                    state[order, 3, first, sign].wait_recv()

    def run(self):
        self.pair_start()
        here = self.open(False)
        self.near(here, False)
        self.opposite(here, False)
        self.relay(here, False, 0)
        self.pair_wait()
        there = self.open(True)
        self.relay(here, False, 1)
        self.relay(here, False, -1)
        self.near(there, True)
        self.relay(here, False, 2)
        self.opposite(there, True)
        self.close(here)
        for first in (0, 1, -1, 2):
            self.relay(there, True, first)
        self.close(there)


class Scatter:
    def __init__(self, place, mail, sums, halves, wholes, pair):
        self.place, self.mail = place, mail
        self.sums, self.halves, self.wholes, self.pair = sums, halves, wholes, pair

    def view(self, chip, order, quarter):
        width = D // 4
        if quarter is None:
            return self.sums.at[chip, :, pl.ds(order * 2 * width, 2 * width)]
        return self.sums.at[chip, :, pl.ds((2 * order + quarter) * width, width)]

    def lines(self, stage):
        return (0, 1, 2, 3) if stage == 0 else (4,)

    def chip(self, order, far, stage, line, second):
        if stage == 0:
            return self.place.along(order, far, line, second)
        return self.place.along(order, far, second, 0)

    def open(self, far, order, stage):
        state = {}
        for line in self.lines(stage):
            chip = self.chip(order, far, stage, line, 2)
            for side, sign in ((0, -1), (1, 1)):
                slot = self.halves.at[int(far), order, line, side]
                state[line, 0, side] = self.mail.send(
                    self.view(chip, order, side), slot, self.place.step(order, 1 - stage, sign)
                )
        return state

    def add(self, chip, order, quarter, terms):
        ref = self.view(chip, order, quarter)
        total = ref[...].astype(F32)
        for term in terms:
            total = total + term[...].astype(F32)
        ref[...] = total.astype(BF)

    def middle(self, state, far, order, stage):
        for line in self.lines(stage):
            for side, sign in ((0, -1), (1, 1)):
                state[line, 0, side].wait_recv()
                chip = self.chip(order, far, stage, line, sign)
                self.add(chip, order, side, [self.halves.at[int(far), order, line, side]])
                slot = self.wholes.at[int(far), order, line, side]
                state[line, 1, side] = self.mail.send(
                    self.view(chip, order, None), slot, self.place.step(order, 1 - stage, sign)
                )

    def close(self, state, far, order, stage):
        for line in self.lines(stage):
            for side in (0, 1):
                state[line, 1, side].wait_recv()
            chip = self.chip(order, far, stage, line, 0)
            self.add(
                chip, order, None, [self.wholes.at[int(far), order, line, side] for side in (0, 1)]
            )


def feed_forward(
    block_ref,
    mlp_gain,
    attn_gain,
    gate_ref,
    up_ref,
    down_ref,
    kv_w_ref,
    cos_ref,
    sin_ref,
    slot_ref,
    out_ref,
    kv_ref,
    tokens,
    first_w,
    down_w,
    kv_w,
    first_acc,
    kv_acc,
    squares,
    hidden,
    sums,
    halves,
    wholes,
    pair_slot,
    kv_all,
    kv_part,
    send_sems,
    recv_sems,
    local_sems,
):
    place = Place()
    mail = Mail(send_sems, recv_sems)
    core = place.core
    mine = place.chip(False, 0, 0)
    other = place.device(False, 0, 0, other_core=True)

    block_copy = pltpu.make_async_copy(block_ref, tokens.at[mine], local_sems.at[0])
    block_copy.start()
    kv_cols = pl.ds(pl.multiple_of(core * HD, HD), HD)
    targets = [
        (gate_ref, first_w.at[core]),
        (up_ref, first_w.at[2 + core]),
        (down_ref, down_w.at[core]),
        (kv_w_ref, kv_w.at[:, kv_cols]),
    ]
    local_copies = []
    for number, (source, target) in enumerate(targets):
        copy = pltpu.make_async_copy(source, target, local_sems.at[1 + number])
        copy.start()
        local_copies.append(copy)
    block_copy.wait()
    greet(place)

    def cut(chip, order, quarter):
        if quarter is None:
            return tokens.at[chip, pl.ds(order * 256, 256)]
        return tokens.at[chip, pl.ds(order * 256 + quarter * 128, 128)]

    gather = Gather(place, mail, cut, lambda chip: tokens.at[chip])
    weight_mail = [mail.send(source, target, other) for source, target in targets]
    gather.run()
    for copy in local_copies:
        copy.wait()
    for copy in weight_mail:
        copy.wait_recv()

    first_acc[...] = jnp.zeros_like(first_acc)
    kv_acc[...] = jnp.zeros_like(kv_acc)
    squares[...] = jnp.zeros_like(squares)
    contract = (((1,), (1,)), ((), ()))

    def accumulate(step, _):
        cols = pl.ds(pl.multiple_of(step * STEP, STEP), STEP)
        rows = jnp.concatenate([tokens[step * 8 + j] for j in range(8)], axis=1).astype(F32)
        part = rows * rows
        for j in range(8):
            squares[...] += part[:, j * 128 : (j + 1) * 128]
        scaled = (rows * mlp_gain[pl.ds(step, 1), :]).astype(BF)
        for part in range(4):
            first_acc[part] += lax.dot_general(
                scaled, first_w[part, :, cols], contract, preferred_element_type=F32
            )
        scaled = (rows * attn_gain[pl.ds(step, 1), :]).astype(BF)
        kv_acc[...] += jnp.dot(scaled, kv_w[cols, :], preferred_element_type=F32)
        return 0

    lax.fori_loop(0, D // STEP, accumulate, 0)
    mean_square = jnp.sum(squares[...], axis=1, keepdims=True) * (1.0 / D)
    inverse = lax.rsqrt(mean_square + 1e-05)
    for part in (0, 1):
        gate_val = first_acc[part] * inverse
        up_val = first_acc[2 + part] * inverse
        hidden[part] = (gate_val / (1.0 + jnp.exp(-gate_val)) * up_val).astype(BF)

    def project(step, _):
        cols = pl.ds(pl.multiple_of(step * 512, 512), 512)
        part = jnp.dot(hidden[0], down_w[0, :, cols], preferred_element_type=F32)
        part = part + jnp.dot(hidden[1], down_w[1, :, cols], preferred_element_type=F32)
        sums[:, :, cols] = part.astype(BF).reshape(CHIPS, OWN, 512)
        return 0

    lax.fori_loop(0, D // 512, project, 0)

    scatter = Scatter(place, mail, sums, halves, wholes, pair_slot)
    keys = (True, 0), (True, 1), (False, 0), (False, 1)
    outer = {key: scatter.open(key[0], key[1], 0) for key in keys}

    turn = kv_acc[...] * inverse
    key_part = turn[:, :HD]
    lane = lax.broadcasted_iota(jnp.int32, key_part.shape, 1)
    partner = jnp.where(
        lax.rem(lane, 2) == 0,
        pltpu.roll(key_part, HD - 1, axis=1),
        pltpu.roll(key_part, 1, axis=1),
    )
    key_part = (key_part * cos_ref[...] + partner * sin_ref[...]).astype(BF)
    value_part = turn[:, HD:].astype(BF)
    my_rows = pl.ds(pl.multiple_of(core * ROWS, ROWS), ROWS)
    first_core = core == 0
    kv_all[my_rows, :] = jnp.where(first_core, key_part, value_part)
    kv_part[...] = jnp.where(first_core, value_part, key_part)
    kv_mail = mail.send(kv_part, kv_all.at[my_rows], other)

    for key in keys:
        scatter.middle(outer[key], key[0], key[1], 0)
    inner = {}
    for key in keys:
        scatter.close(outer[key], key[0], key[1], 0)
        inner[key] = scatter.open(key[0], key[1], 1)
    kv_mail.wait_recv()
    pick = lax.broadcasted_iota(jnp.int32, (ROWS, 2 * ROWS), 1) == slot_ref[...]
    kv_ref[...] = jnp.dot(
        pick.astype(F32).astype(BF), kv_all[...], preferred_element_type=F32
    ).astype(BF)
    for key in keys:
        scatter.middle(inner[key], key[0], key[1], 1)
    for key in keys[:2]:
        scatter.close(inner[key], key[0], key[1], 1)
    pair_mail = mail.send(
        sums.at[place.chip(True, 0, 0)], pair_slot, place.device(True, 0, 0)
    )
    for key in keys[2:]:
        scatter.close(inner[key], key[0], key[1], 1)
    own_rows = pl.ds(pl.multiple_of(mine * OWN, OWN), OWN)
    pair_mail.wait_recv()
    for chip in range(CHIPS):
        cols = slice(chip * 128, (chip + 1) * 128)
        mixed = sums[mine, :, cols].astype(F32) + pair_slot[:, cols].astype(F32)
        out_ref[:, cols] = (tokens[chip, own_rows, :].astype(F32) + mixed).astype(BF)
    mail.finish()


def feed_forward_call(block, mlp_gain, attn_gain, gate_t, up_t, down, kv_w, cosine, sine, slot_row):
    anywhere = pl.BlockSpec(memory_space=pl.ANY)
    local = pl.BlockSpec(memory_space=pltpu.VMEM)
    return pl.pallas_call(
        feed_forward,
        out_shape=(
            jax.ShapeDtypeStruct((OWN, D), BF),
            jax.ShapeDtypeStruct((ROWS, HD), BF),
        ),
        in_specs=[anywhere, local, local, anywhere, anywhere, anywhere, anywhere, local, local, local],
        out_specs=(local, local),
        scratch_shapes=[
            pltpu.VMEM((CHIPS, ROWS, 128), BF),
            pltpu.VMEM((4, UNITS, D), BF),
            pltpu.VMEM((2, UNITS, D), BF),
            pltpu.VMEM((D, 2 * HD), BF),
            pltpu.VMEM((4, ROWS, UNITS), F32),
            pltpu.VMEM((ROWS, 2 * HD), F32),
            pltpu.VMEM((ROWS, 128), F32),
            pltpu.VMEM((2, ROWS, UNITS), BF),
            pltpu.VMEM((CHIPS, OWN, D), BF),
            pltpu.VMEM((2, 2, 5, 2, OWN, D // 4), BF),
            pltpu.VMEM((2, 2, 5, 2, OWN, D // 2), BF),
            pltpu.VMEM((OWN, D), BF),
            pltpu.VMEM((2 * ROWS, HD), BF),
            pltpu.VMEM((ROWS, HD), BF),
            pltpu.SemaphoreType.DMA((176,)),
            pltpu.SemaphoreType.DMA((176,)),
            pltpu.SemaphoreType.DMA((5,)),
        ],
        compiler_params=pltpu.CompilerParams(
            collective_id=1, has_side_effects=True, vmem_limit_bytes=63 * 1024 * 1024
        ),
        name="feed_forward",
    )(block, mlp_gain, attn_gain, gate_t, up_t, down, kv_w, cosine, sine, slot_row)


def own_core_tokens(core):
    local_row = jnp.arange(ROWS, dtype=jnp.int32)
    return (local_row // OWN * 2 + core) * OWN + local_row % OWN


def local(
    patches,
    grids,
    positions,
    vis_gain,
    vis_query,
    vis_key,
    vis_value,
    vis_out,
    w_proj,
    text_embed,
    slots,
    lengths,
    attn_gain,
    mlp_gain,
    w_kv,
    w_gate,
    w_up,
    w_down,
):
    segment, corners = image_tables(grids[0])
    normed = layer_norm(patches, vis_gain)
    query_rows = jnp.dot(normed, vis_query, preferred_element_type=jnp.float32).astype(jnp.bfloat16)
    key_rows = jnp.dot(normed, vis_key, preferred_element_type=jnp.float32).astype(jnp.bfloat16)
    value_rows = jnp.dot(normed, vis_value, preferred_element_type=jnp.float32).astype(jnp.bfloat16)
    slot_count = patches.shape[0]
    head_count = query_rows.shape[1] // VHD
    head_query = query_rows.reshape(slot_count, head_count, VHD)
    head_key = key_rows.reshape(slot_count, head_count, VHD)
    head_value = value_rows.reshape(slot_count, head_count, VHD)
    scores = jnp.einsum(
        "qhd,khd->hqk", head_query, head_key, preferred_element_type=jnp.float32
    ) * VHD ** (-0.5)
    allowed = segment[:, None] == segment[None, :]
    scores = jnp.where(allowed[None, :, :], scores, -1e30)
    row_max = jnp.max(scores, axis=-1, keepdims=True)
    expos = jnp.exp(scores - row_max)
    attn_probs = (expos / jnp.sum(expos, axis=-1, keepdims=True)).astype(jnp.bfloat16)
    context = jnp.einsum("hqk,khd->qhd", attn_probs, head_value, preferred_element_type=jnp.float32)
    context = context.reshape(slot_count, head_count * VHD).astype(jnp.bfloat16)
    partial_out = jnp.dot(context, vis_out, preferred_element_type=jnp.float32)
    attended = lax.psum(partial_out.astype(jnp.bfloat16), "grp").astype(jnp.float32)
    vision = (patches.astype(jnp.float32) + attended).astype(jnp.bfloat16)
    merged = vision[corners.reshape(-1)].reshape(corners.shape[0], 4 * patches.shape[1])
    tok_dev = text_embed.shape[0]
    tp_count = lax.axis_size("tp")
    half_tok = tok_dev * tp_count
    group_index = lax.axis_index("grp")
    tp_index = lax.axis_index("tp")
    core = tp_index % 2
    col_count = w_proj.shape[1]
    image_cols = jnp.dot(
        lax.all_gather(merged, "tp", axis=0, tiled=True), w_proj, preferred_element_type=jnp.float32
    ).astype(jnp.bfloat16)
    local_rows = positions - group_index * half_tok
    inside = (local_rows >= 0) & (local_rows < half_tok)
    local_rows = jnp.where(inside, local_rows, half_tok)
    buffer = (
        jnp.zeros((half_tok, col_count), jnp.bfloat16).at[local_rows].set(image_cols, mode="drop")
    )
    is_image = jnp.zeros((half_tok,), jnp.int32).at[local_rows].set(1, mode="drop")
    text_cols = lax.all_to_all(text_embed, "tp", split_axis=1, concat_axis=0, tiled=True)
    columns = jnp.where(is_image[:, None] > 0, buffer, text_cols)
    by_core = columns.reshape(tp_count // 2, 2, tok_dev, col_count)
    mine = lax.dynamic_index_in_dim(by_core, core, 1, keepdims=False).reshape(ROWS, col_count)
    theirs = lax.dynamic_index_in_dim(by_core, 1 - core, 1, keepdims=False).reshape(ROWS, col_count)
    swap = [(index, index ^ 1) for index in range(tp_count)]
    came = lax.ppermute(theirs, "tp", swap)
    block = jnp.where(
        core == 0, jnp.concatenate([mine, came], 1), jnp.concatenate([came, mine], 1)
    )

    token_pos = slot_positions(own_core_tokens(core), lengths[0])
    cosine, sine = rotation_tables(token_pos)
    slot_ids = slots[0]
    slot_row = slot_ids // OWN % 2 * ROWS + slot_ids // (2 * OWN) * OWN + slot_ids % OWN
    layer_out, kv_out = feed_forward_call(
        block,
        mlp_gain.reshape(D // STEP, STEP),
        attn_gain.reshape(D // STEP, STEP),
        w_gate.T,
        w_up.T,
        w_down,
        w_kv,
        cosine,
        sine,
        slot_row[:, None],
    )
    return (layer_out, kv_out[None])


def solution(mesh):
    return jax.shard_map(
        local,
        mesh=mesh,
        in_specs=(
            P("tp", None),
            P("tp", None, None),
            P(),
            P(),
            P(None, "grp"),
            P(None, "grp"),
            P(None, "grp"),
            P("grp", None),
            P(None, "tp"),
            P(("grp", "tp"), None),
            P("grp", None),
            P("grp", None),
            P(),
            P(),
            P(None, "tp"),
            P(None, "tp"),
            P(None, "tp"),
            P("tp", None),
        ),
        out_specs=(P(("grp", "tp"), None), P("grp", None, "tp")),
        check_vma=False,
    )
```
